32 devices in a mesh: expert: 2 (over x), context: 4 (over z), dp: 4 (over y, core).
Axes of the slice: x: 2, y: 2, z: 4, core: 2. Of those that a mesh axis runs over, the one named last changes fastest.
Arguments:
- tokens: bfloat16 [2, 8, 1024, 768], P(None, ('expert', 'dp'), 'context'), may hold values from -6 to 6
- lengths: int32 [2, 8], P(None, ('expert', 'dp')), may hold values from 512 to 1024, as said below
- routes: int32 [2, 8, 1024, 2], P(None, ('expert', 'dp'), 'context'), may hold values from 0 to 7, all different within a row
- attn_gain: bfloat16 [768], replicated, may hold values from 0.5 to 1.5
- w_query: bfloat16 [768, 768], replicated, may hold values from -0.21875 to 0.21875
- w_key: bfloat16 [768, 768], replicated, may hold values from -0.21875 to 0.21875
- w_value: bfloat16 [768, 768], replicated, may hold values from -0.21875 to 0.21875
- w_output: bfloat16 [768, 768], replicated, may hold values from -1.75 to 1.75
- rel_bias: bfloat16 [12, 32], replicated, may hold values from -4 to 4
- ffn_gain: bfloat16 [768], replicated, may hold values from 0.5 to 1.5
- w_router: bfloat16 [768, 8], replicated, may hold values from -0.21875 to 0.21875
- w_in: bfloat16 [8, 768, 3072], P(('expert', 'dp'), None, 'context'), may hold values from -0.21875 to 0.21875
- w_out: bfloat16 [8, 3072, 768], P(('expert', 'dp'), 'context'), may hold values from -0.109375 to 0.109375
- out_grad: bfloat16 [2, 8, 1024, 768], P(None, ('expert', 'dp'), 'context'), may hold values from -6 to 6
Outputs:
- block_out: bfloat16 [2, 8, 1024, 768], P(None, ('expert', 'dp'), 'context')
- tokens_grad: float32 [2, 8, 1024, 768], P(None, ('expert', 'dp'), 'context')
- attn_gain_grad: float32 [768], replicated
- w_query_grad: float32 [768, 768], replicated
- w_key_grad: float32 [768, 768], replicated
- w_value_grad: float32 [768, 768], replicated
- w_output_grad: float32 [768, 768], replicated
- rel_bias_grad: float32 [12, 32], replicated
- ffn_gain_grad: float32 [768], replicated
- w_router_grad: float32 [768, 8], replicated
- w_in_grad: float32 [8, 768, 3072], P(('expert', 'dp'), None, 'context')
- w_out_grad: float32 [8, 3072, 768], P(('expert', 'dp'), 'context')
The draws below stay inside these ranges and needn't reach their ends.
Inputs may be any that keep to these rules, and one draw needn't show every extreme that they name: `lengths`: every micro-batch holds a slot of length 1024 and one of length 512. `routes`: the two experts of a position differ.
All inputs are finite; a program needn't handle non-finite values.
Results may differ from the reference program's by a relative error of at most 0.017.
Values may be sent and summed in bfloat16 or wider, within the bound.
A program may use at most 256 MiB of HBM per device.

```python
import jax
import jax.numpy as jnp
import numpy as np
from jax import lax

D = 768
HEADS = 12
HEAD_DIM = 64
FF = 3072
BUCKETS = 32
MAX_DIST = 128
TOP_K = 2
SEQ = 1024
MICRO = 2
SLOTS = 8
EXPERTS = 8
CTX = 256
CAP = 80
N_CONTEXT = 4


def draw_lengths(key, part):
    drawn = jax.random.randint(key, (MICRO, SLOTS), SEQ // 2, SEQ + 1, dtype=jnp.int32)
    drawn = drawn.at[:, 0].set(SEQ)
    return drawn.at[:, 1].set(SEQ // 2)


def block_scale(stream_key, extent, split, low, largest):
    level = 1.0
    for position, blocks in split:
        draws = jax.random.uniform(jax.random.fold_in(jax.random.fold_in(stream_key, 6), position), (blocks,), jnp.float32, low / len(split), largest / len(split))
        level = level * jnp.repeat(jnp.exp(draws), extent[position] // blocks).reshape((-1,) + (1,) * (len(extent) - 1 - position))
    return level


def different_ones(key, rows, amount, top, lift):
    ranking = jax.random.permutation(jax.random.fold_in(key, 1), amount)
    boost = ranking
    for power in range(3):
        boost = boost * boost // amount
    boost = boost * lift // amount
    lots = jax.random.randint(jax.random.fold_in(key, 2), (rows, amount), 0, 4096) + boost
    holders = jax.random.permutation(jax.random.fold_in(key, 3), rows)[jnp.arange(amount) % rows]
    lots = jnp.where(jnp.arange(rows)[:, None] == holders[None, :], 1 << 14, lots)
    priority = lots * amount + jnp.arange(amount)
    return lax.top_k(priority.astype(jnp.int32), top)[1].astype(jnp.int32)


def scatter_about(rng, shape, scale, reach, cuts=(), held_as=jnp.bfloat16):
    loudness = block_scale(rng, shape, cuts, -0.22, 0.18) if cuts else 1.0
    entries = jax.random.normal(rng, shape, jnp.float32) * scale * loudness
    return jnp.minimum(jnp.maximum(entries, -reach), reach).astype(held_as)


def setup_inputs(seed: int = 0) -> dict:
    streams_of = jax.random.split(jax.random.key(seed), 15)
    tokens = scatter_about(streams_of[0], (MICRO, SLOTS, SEQ, D), 1.0, 6.0, ((1, 8), (2, 4)))
    lengths = draw_lengths(jax.random.fold_in(streams_of[14], 71), 0)
    routes = different_ones(streams_of[2], MICRO * SLOTS * SEQ, EXPERTS, TOP_K, 2048).reshape((MICRO, SLOTS, SEQ, TOP_K))
    attn_gain = jnp.clip(1.0 + 0.1 * jax.random.normal(streams_of[3], (D,), jnp.float32), 0.5, 1.5).astype(jnp.bfloat16)
    w_query = scatter_about(streams_of[4], (D, D), D ** -0.5, 0.21875)
    w_key = scatter_about(streams_of[5], (D, D), D ** -0.5, 0.21875)
    w_value = scatter_about(streams_of[6], (D, D), D ** -0.5, 0.21875)
    w_output = scatter_about(streams_of[7], (D, D), (max(1, D // 64)) ** -0.5, 1.75)
    rel_bias = scatter_about(streams_of[8], (HEADS, BUCKETS), 1.0, 4.0)
    ffn_gain = jnp.clip(1.0 + 0.1 * jax.random.normal(streams_of[9], (D,), jnp.float32), 0.5, 1.5).astype(jnp.bfloat16)
    w_router = scatter_about(streams_of[10], (D, EXPERTS), D ** -0.5, 0.21875)
    w_in = scatter_about(streams_of[11], (EXPERTS, D, FF), D ** -0.5, 0.21875, ((0, 8), (2, 4)))
    w_out = scatter_about(streams_of[12], (EXPERTS, FF, D), FF ** -0.5, 0.109375, ((0, 8), (1, 4)))
    out_grad = scatter_about(streams_of[13], (MICRO, SLOTS, SEQ, D), 1.0, 6.0, ((1, 8), (2, 4)))
    return {"tokens": tokens, "lengths": lengths, "routes": routes, "attn_gain": attn_gain, "w_query": w_query, "w_key": w_key, "w_value": w_value, "w_output": w_output, "rel_bias": rel_bias, "ffn_gain": ffn_gain, "w_router": w_router, "w_in": w_in, "w_out": w_out, "out_grad": out_grad}


EPSILON = 1e-06
BEST_PRECISION = lax.Precision.HIGHEST

@jax.custom_vjp
def low(v):
    return lax.optimization_barrier(v.astype(jnp.bfloat16)).astype(jnp.float32)

@jax.custom_vjp
def low_back(v):
    return v

def low_keep(v):
    return (low(v), None)

def low_pass(kept, grad):
    return (grad,)

def back_keep(v):
    return (v, None)

def back_low(kept, grad):
    return (low(grad),)
low.defvjp(low_keep, low_pass)
low_back.defvjp(back_keep, back_low)

def bucket_table(buckets, far):
    exact_count = buckets // 2
    distance = np.arange(far + 1)
    safe_dist = np.maximum(distance, 1)
    log_bucket = exact_count + np.floor(np.log(safe_dist / exact_count) / np.log(far / exact_count) * (buckets - exact_count)).astype(np.int64)
    bucket_ids = np.where(distance < exact_count, distance, np.minimum(log_bucket, buckets - 1))
    return (bucket_ids[None, :] == np.arange(buckets)[:, None]).astype(np.float32)

def norm_rows(values, gain):
    row_scale = lax.rsqrt(lax.optimization_barrier(jnp.mean(values * values, axis=-1, keepdims=True)) + EPSILON)
    return values * row_scale * gain

def gate_weights(logits, route_ids, experts):
    probs = jax.nn.softmax(logits, axis=-1)
    chosen = (route_ids[..., :, None] == jnp.arange(experts, dtype=jnp.int32)).astype(jnp.float32)
    picked = lax.optimization_barrier(jnp.sum(probs[..., None, :] * chosen, axis=-1))
    return picked / lax.optimization_barrier(jnp.sum(picked, axis=-1, keepdims=True))

def slot_places(route_ids, valid_rows, experts, capacity):
    pair_order = jnp.concatenate([route_ids[..., 0], route_ids[..., 1]], axis=-1)
    pair_live = jnp.concatenate([valid_rows, valid_rows], axis=-1)
    chosen = ((pair_order[..., None] == jnp.arange(experts, dtype=jnp.int32)) & pair_live[..., None]).astype(jnp.int32)
    counts = jnp.cumsum(chosen, axis=-2)
    place_idx = lax.optimization_barrier(jnp.sum(counts * chosen, axis=-1)) - 1
    pair_kept = pair_live & (place_idx < capacity)
    return jnp.where(pair_kept, pair_order * capacity + place_idx, -1).astype(jnp.int32)

def slot_forward(params, token_row, length, route_row):
    attn_gain, w_query, w_key, w_value, w_output, rel_bias, ffn_gain, w_router, w_in, w_out = params
    positions = jnp.arange(SEQ, dtype=jnp.int32)
    valid_rows = positions < length
    normed = low(norm_rows(token_row, attn_gain))

    def project(weight):
        return low(low_back(jnp.dot(normed, weight, precision=BEST_PRECISION))).reshape(SEQ, HEADS, HEAD_DIM)
    queries = project(w_query)
    key_rows = project(w_key)
    value_rows = project(w_value)
    bias_far = jnp.dot(rel_bias, jnp.asarray(bucket_table(BUCKETS, MAX_DIST)), precision=BEST_PRECISION)
    block_rows = min(512, SEQ)
    score_scale = HEAD_DIM ** (-0.5)

    def attend(block_id):
        offset = block_id * block_rows
        query_block = lax.dynamic_slice_in_dim(queries, offset, block_rows, 0)
        query_pos = offset + jnp.arange(block_rows, dtype=jnp.int32)
        scores = jnp.einsum('qhd,khd->hqk', query_block, key_rows, precision=BEST_PRECISION) * score_scale
        distance = jnp.clip(query_pos[:, None] - positions[None, :], 0, MAX_DIST)
        scores = low_back(scores + jnp.take(bias_far, distance, axis=1))
        allowed = (positions[None, :] <= query_pos[:, None]) & valid_rows[None, :]
        weights = jnp.where(allowed[None], jnp.exp(scores), 0.0)
        totals = lax.optimization_barrier(jnp.sum(weights, axis=-1))
        mixed_rows = low_back(jnp.einsum('hqk,khd->qhd', low(weights), value_rows, precision=BEST_PRECISION))
        return mixed_rows / jnp.transpose(totals)[:, :, None]
    attended = lax.map(jax.checkpoint(attend), jnp.arange(SEQ // block_rows, dtype=jnp.int32))
    attended = low(attended.reshape(SEQ, D))
    branch = low_back(jnp.dot(attended, w_output, precision=BEST_PRECISION))
    hidden_one = token_row + branch
    routed = low(norm_rows(hidden_one, ffn_gain))
    logits = low_back(jnp.dot(routed, w_router, precision=BEST_PRECISION))
    gate_values = gate_weights(logits, route_row, EXPERTS)
    slot_ids = slot_places(route_row.reshape(N_CONTEXT, CTX, 2), valid_rows.reshape(N_CONTEXT, CTX), EXPERTS, CAP)
    places = (slot_ids[..., None] == jnp.arange(EXPERTS * CAP, dtype=jnp.int32)).astype(jnp.float32)
    grouped = routed.reshape(N_CONTEXT, CTX, D)
    doubled = jnp.concatenate([grouped, grouped], axis=1)
    expert_rows = low_back(jnp.einsum('gtn,gtd->gnd', places, doubled, precision=BEST_PRECISION)).reshape(N_CONTEXT, EXPERTS, CAP, D)
    pre_act = low_back(jnp.einsum('gecd,edf->gecf', expert_rows, w_in, precision=BEST_PRECISION))
    activated = low(jax.nn.gelu(pre_act))
    expert_out = low_back(low(jnp.einsum('gecf,efd->gecd', activated, w_out, precision=BEST_PRECISION)))
    returned = jnp.einsum('gtn,gnd->gtd', places, expert_out.reshape(N_CONTEXT, EXPERTS * CAP, D), precision=BEST_PRECISION)
    first_out = returned[:, :CTX].reshape(SEQ, D)
    second_out = returned[:, CTX:].reshape(SEQ, D)
    mixture = gate_values[:, 0:1] * first_out + gate_values[:, 1:2] * second_out
    return jnp.where(valid_rows[:, None], hidden_one + mixture, 0.0)

def reference(tokens, lengths, routes, attn_gain, w_query, w_key, w_value, w_output, rel_bias, ffn_gain, w_router, w_in, w_out, out_grad):
    params = tuple((weight.astype(jnp.float32) for weight in (attn_gain, w_query, w_key, w_value, w_output, rel_bias, ffn_gain, w_router, w_in, w_out)))
    slot_total = MICRO * SLOTS
    token_rows = tokens.reshape(slot_total, SEQ, D).astype(jnp.float32)
    grad_rows = out_grad.reshape(slot_total, SEQ, D).astype(jnp.float32)
    length_rows = lengths.reshape(slot_total)
    route_rows = routes.reshape(slot_total, SEQ, 2)

    def visit(grad_sums, slot_item):
        token_row, length, route_row, grad_row = slot_item
        result, pull_back = jax.vjp(lambda weights, inputs: slot_forward(weights, inputs, length, route_row), params, token_row)
        weight_grads, input_grad = pull_back(grad_row)
        grad_sums = jax.tree.map(lambda running, update: running + update, grad_sums, weight_grads)
        return (grad_sums, (result.astype(jnp.bfloat16), input_grad))
    start_sums = jax.tree.map(jnp.zeros_like, params)
    grad_sums, (outputs, input_grads) = lax.scan(visit, start_sums, (token_rows, length_rows, route_rows, grad_rows))
    return (outputs.reshape(MICRO, SLOTS, SEQ, D), input_grads.reshape(MICRO, SLOTS, SEQ, D), grad_sums[0], grad_sums[1], grad_sums[2], grad_sums[3], grad_sums[4], grad_sums[5], grad_sums[6], grad_sums[7], grad_sums[8], grad_sums[9])
```

```python
import functools

import jax
import jax.numpy as jnp
import numpy as np
from jax import lax
from jax.experimental import pallas as pl
from jax.experimental.pallas import tpu as pltpu
from jax.sharding import PartitionSpec as P

MAX_DIST = 128


EPSILON = 1e-06
BEST_PRECISION = lax.Precision.HIGHEST


def bucket_table(buckets, far):
    exact_count = buckets // 2
    distance = np.arange(far + 1)
    safe_dist = np.maximum(distance, 1)
    log_bucket = exact_count + np.floor(
        np.log(safe_dist / exact_count) / np.log(far / exact_count) * (buckets - exact_count)
    ).astype(np.int64)
    bucket_ids = np.where(distance < exact_count, distance, np.minimum(log_bucket, buckets - 1))
    return (bucket_ids[None, :] == np.arange(buckets)[:, None]).astype(np.float32)


def gate_weights(logits, route_ids, experts):
    probs = jax.nn.softmax(logits, axis=-1)
    chosen = (route_ids[..., :, None] == jnp.arange(experts, dtype=jnp.int32)).astype(jnp.float32)
    picked = jnp.sum(probs[..., None, :] * chosen, axis=-1)
    return picked / jnp.sum(picked, axis=-1, keepdims=True)


def slot_places(route_ids, valid_rows, experts, capacity):
    pair_order = jnp.concatenate([route_ids[..., 0], route_ids[..., 1]], axis=-1)
    pair_live = jnp.concatenate([valid_rows, valid_rows], axis=-1)
    chosen = (
        (pair_order[..., None] == jnp.arange(experts, dtype=jnp.int32)) & pair_live[..., None]
    ).astype(jnp.int32)
    counts = jnp.cumsum(chosen, axis=-2)
    place_idx = jnp.sum(counts * chosen, axis=-1) - 1
    pair_kept = pair_live & (place_idx < capacity)
    return jnp.where(pair_kept, pair_order * capacity + place_idx, -1)


def band_bias(bias_far, query_start, query_count, key_count):
    far_limit = bias_far.shape[1] - 1
    span = query_count + key_count - 1
    steps = jnp.arange(span, dtype=jnp.int32)
    differ = query_start + jnp.where(steps < key_count, -steps, span - steps)
    picks = jnp.clip(differ, 0, far_limit)
    select = (picks[:, None] == jnp.arange(far_limit + 1, dtype=jnp.int32)[None, :]).astype(
        jnp.float32
    )
    vector = jnp.dot(bias_far, jnp.transpose(select), precision=BEST_PRECISION)
    tiled = jnp.tile(vector, (1, query_count))[:, : query_count * (span - 1)]
    return tiled.reshape(bias_far.shape[0], query_count, span - 1)[:, :, :key_count]


def score_block(queries, key_part, query_pos, slot_len, bias_far, score_scale):
    key_count = key_part.shape[1]
    query_count = query_pos.shape[0]
    key_pos = jnp.arange(key_count, dtype=jnp.int32)
    scores = (
        jnp.einsum("bchd,bkhd->bhck", queries, key_part, preferred_element_type=jnp.float32)
        * score_scale
    )
    scores = scores + band_bias(bias_far, query_pos[0], query_count, key_count)[None]
    causal = (key_pos[None, :] <= query_pos[:, None])[None, None]
    inside = (key_pos[None, :] < slot_len[:, None])[:, None, None, :]
    return jnp.where(causal & inside, jnp.exp(scores), 0.0)


def diagonal_bins(grad_scores, query_start, bin_count):
    head_count, query_count, key_count = grad_scores.shape
    width = key_count + query_count
    padded = jnp.pad(grad_scores, ((0, 0), (0, 0), (query_count, 0)))
    flat_rows = padded.reshape(head_count, query_count * width)
    flat_rows = jnp.pad(flat_rows, ((0, 0), (0, query_count)))
    skewed = flat_rows.reshape(head_count, query_count, width + 1)
    diag_sums = jnp.sum(skewed, axis=1)
    distance = query_start + query_count - jnp.arange(width + 1, dtype=jnp.int32)
    bin_ids = jnp.arange(bin_count, dtype=jnp.int32)
    bin_select = (distance[:, None] == bin_ids[None, :]) | (distance[:, None] >= bin_count - 1) & (
        bin_ids[None, :] == bin_count - 1
    )
    return jnp.dot(diag_sums, bin_select.astype(jnp.float32), precision=BEST_PRECISION)


def norm_back(grad_normed, values, row_scale, gain):
    scaled = grad_normed * gain
    cubed = row_scale * row_scale * row_scale
    return row_scale * scaled - values * cubed * jnp.mean(scaled * values, axis=-1, keepdims=True)


def local(
    tokens,
    lengths,
    routes,
    attn_gain,
    w_query,
    w_key,
    w_value,
    w_output,
    rel_bias,
    ffn_gain,
    w_router,
    w_in,
    w_out,
    out_grad,
):
    micro_count, slots_here, rows_dev, model_width = tokens.shape
    head_count, buckets = rel_bias.shape
    head_dim = model_width // head_count
    score_scale = head_dim ** (-0.5)
    experts = w_router.shape[1]
    capacity = max(2, 5 * rows_dev // (2 * experts))
    query_pos = lax.axis_index("context") * rows_dev + jnp.arange(rows_dev, dtype=jnp.int32)
    far_table = jnp.asarray(bucket_table(buckets, MAX_DIST))
    bias_far = jnp.dot(rel_bias.astype(jnp.float32), far_table, precision=BEST_PRECISION)
    gain_one = attn_gain.astype(jnp.float32)
    gain_two = ffn_gain.astype(jnp.float32)
    in_local = w_in[0]
    out_local = w_out[0]
    grad_in_acc = jnp.zeros(in_local.shape, jnp.float32)
    grad_out_acc = jnp.zeros(out_local.shape, jnp.float32)
    grad_gain_one = jnp.zeros((model_width,), jnp.float32)
    grad_gain_two = jnp.zeros((model_width,), jnp.float32)
    grad_query = jnp.zeros((model_width, model_width), jnp.float32)
    grad_key = jnp.zeros((model_width, model_width), jnp.float32)
    grad_value = jnp.zeros((model_width, model_width), jnp.float32)
    grad_output_w = jnp.zeros((model_width, model_width), jnp.float32)
    grad_router = jnp.zeros((model_width, experts), jnp.float32)
    grad_bias_far = jnp.zeros(bias_far.shape, jnp.float32)
    block_outputs = []
    input_grads = []
    shape_heads = (slots_here, rows_dev, head_count, head_dim)
    for micro_idx in range(micro_count):
        inputs = tokens[micro_idx].astype(jnp.float32)
        slot_len = lengths[micro_idx]
        route_ids = routes[micro_idx]
        valid_rows = query_pos[None, :] < slot_len[:, None]
        live_rows = valid_rows[..., None].astype(jnp.float32)
        scale_one = lax.rsqrt(jnp.mean(inputs * inputs, axis=-1, keepdims=True) + EPSILON)
        normed = (inputs * scale_one * gain_one).astype(jnp.bfloat16)
        queries = (
            jnp.einsum("bcd,de->bce", normed, w_query, preferred_element_type=jnp.float32)
            .astype(jnp.bfloat16)
            .reshape(shape_heads)
        )
        key_rows = (
            jnp.einsum("bcd,de->bce", normed, w_key, preferred_element_type=jnp.float32)
            .astype(jnp.bfloat16)
            .reshape(shape_heads)
        )
        value_rows = (
            jnp.einsum("bcd,de->bce", normed, w_value, preferred_element_type=jnp.float32)
            .astype(jnp.bfloat16)
            .reshape(shape_heads)
        )
        key_part = lax.all_gather(key_rows, "context", axis=1, tiled=True)
        value_part = lax.all_gather(value_rows, "context", axis=1, tiled=True)
        weights = score_block(queries, key_part, query_pos, slot_len, bias_far, score_scale)
        totals = jnp.sum(weights, axis=-1)
        mixed_acc = jnp.einsum(
            "bhck,bkhd->bchd",
            weights.astype(jnp.bfloat16),
            value_part,
            preferred_element_type=jnp.float32,
        )
        mixed_acc, totals = (mixed_acc, totals)
        inverse = 1.0 / jnp.transpose(totals, (0, 2, 1))[..., None]
        attended_full = mixed_acc * inverse
        attended = attended_full.astype(jnp.bfloat16).reshape(slots_here, rows_dev, model_width)
        hidden_one = inputs + jnp.einsum(
            "bcd,de->bce", attended, w_output, preferred_element_type=jnp.float32
        )
        scale_two = lax.rsqrt(jnp.mean(hidden_one * hidden_one, axis=-1, keepdims=True) + EPSILON)
        routed = (hidden_one * scale_two * gain_two).astype(jnp.bfloat16)
        logits = jnp.einsum("bcd,de->bce", routed, w_router, preferred_element_type=jnp.float32)
        gate_values, gate_pull = jax.vjp(
            lambda logit_rows: gate_weights(logit_rows, route_ids, experts), logits
        )
        slot_ids = slot_places(route_ids, valid_rows, experts, capacity)
        places = (slot_ids[..., None] == jnp.arange(experts * capacity, dtype=jnp.int32)).astype(
            jnp.bfloat16
        )
        doubled = jnp.concatenate([routed, routed], axis=1)
        buffer = jnp.einsum(
            "btn,btd->nbd", places, doubled, preferred_element_type=jnp.float32
        ).astype(jnp.bfloat16)
        buffer = buffer.reshape(experts, capacity * slots_here, model_width)
        received = lax.all_to_all(
            buffer, ("expert", "dp"), split_axis=0, concat_axis=1, tiled=True
        )[0]
        rows_all = lax.all_gather(received, "context", axis=0, tiled=True)
        pre_act = jnp.dot(rows_all, in_local, preferred_element_type=jnp.float32)
        activated = jax.nn.gelu(pre_act).astype(jnp.bfloat16)
        expert_result = lax.psum_scatter(
            jnp.dot(activated, out_local, preferred_element_type=jnp.float32).astype(jnp.bfloat16),
            "context",
            scatter_dimension=0,
            tiled=True,
        )
        returned_back = lax.all_to_all(
            expert_result[None], ("expert", "dp"), split_axis=1, concat_axis=0, tiled=True
        )
        returned = jnp.einsum(
            "btn,nbd->btd",
            places,
            returned_back.reshape(experts * capacity, slots_here, model_width),
            preferred_element_type=jnp.float32,
        )
        first_out = returned[:, :rows_dev]
        second_out = returned[:, rows_dev:]
        mixture = gate_values[..., 0:1] * first_out + gate_values[..., 1:2] * second_out
        block_outputs.append((live_rows * (hidden_one + mixture)).astype(jnp.bfloat16))
        grad_out = out_grad[micro_idx].astype(jnp.float32) * live_rows
        grad_gates = jnp.stack(
            [jnp.sum(grad_out * first_out, axis=-1), jnp.sum(grad_out * second_out, axis=-1)],
            axis=-1,
        )
        weighted = jnp.concatenate(
            [gate_values[..., 0:1] * grad_out, gate_values[..., 1:2] * grad_out], axis=1
        )
        grad_buffer = jnp.einsum(
            "btn,btd->nbd", places.astype(jnp.float32), weighted, precision=BEST_PRECISION
        ).astype(jnp.bfloat16)
        grad_buffer = grad_buffer.reshape(experts, capacity * slots_here, model_width)
        grad_received = lax.all_to_all(
            grad_buffer, ("expert", "dp"), split_axis=0, concat_axis=1, tiled=True
        )[0]
        grad_all = lax.all_gather(grad_received, "context", axis=0, tiled=True)
        grad_act = jnp.einsum("rd,fd->rf", grad_all, out_local, preferred_element_type=jnp.float32)
        grad_pre = jax.vjp(jax.nn.gelu, pre_act)[1](grad_act)[0].astype(jnp.bfloat16)
        grad_out_acc = grad_out_acc + jnp.einsum(
            "rf,rd->fd", activated, grad_all, preferred_element_type=jnp.float32
        )
        grad_in_acc = grad_in_acc + jnp.einsum(
            "rd,rf->df", rows_all, grad_pre, preferred_element_type=jnp.float32
        )
        grad_rows_local = lax.psum_scatter(
            jnp.einsum("rf,df->rd", grad_pre, in_local, preferred_element_type=jnp.float32).astype(
                jnp.bfloat16
            ),
            "context",
            scatter_dimension=0,
            tiled=True,
        )
        grad_back = lax.all_to_all(
            grad_rows_local[None], ("expert", "dp"), split_axis=1, concat_axis=0, tiled=True
        )
        grad_doubled = jnp.einsum(
            "btn,nbd->btd",
            places,
            grad_back.reshape(experts * capacity, slots_here, model_width),
            preferred_element_type=jnp.float32,
        )
        grad_logits = gate_pull(grad_gates)[0].astype(jnp.bfloat16)
        grad_router = grad_router + jnp.einsum(
            "bcd,bce->de", routed, grad_logits, preferred_element_type=jnp.float32
        )
        grad_routed = (
            grad_doubled[:, :rows_dev]
            + grad_doubled[:, rows_dev:]
            + jnp.einsum("bce,de->bcd", grad_logits, w_router, preferred_element_type=jnp.float32)
        )
        grad_gain_two = grad_gain_two + jnp.sum(grad_routed * hidden_one * scale_two, axis=(0, 1))
        grad_hidden = grad_out + norm_back(grad_routed, hidden_one, scale_two, gain_two)
        grad_branch = grad_hidden.astype(jnp.bfloat16)
        grad_output_w = grad_output_w + jnp.einsum(
            "bcd,bce->de", attended, grad_branch, preferred_element_type=jnp.float32
        )
        grad_attended = jnp.einsum(
            "bce,de->bcd", grad_branch, w_output, preferred_element_type=jnp.float32
        ).reshape(shape_heads)
        grad_mixed = (grad_attended * inverse).astype(jnp.bfloat16)
        grad_totals = (
            -jnp.transpose(jnp.sum(grad_attended * attended_full, axis=-1), (0, 2, 1)) / totals
        )
        grad_far = jnp.zeros(bias_far.shape, jnp.float32)
        backward_key_part = lax.all_gather(key_rows, "context", axis=1, tiled=True)
        backward_value_part = lax.all_gather(value_rows, "context", axis=1, tiled=True)
        key_count = backward_key_part.shape[1]
        backward_weights = score_block(
            queries, backward_key_part, query_pos, slot_len, bias_far, score_scale
        )
        grad_weights = (
            jnp.einsum(
                "bchd,bkhd->bhck",
                grad_mixed,
                backward_value_part,
                preferred_element_type=jnp.float32,
            )
            + grad_totals[..., None]
        )
        grad_scores = (grad_weights * backward_weights).astype(jnp.bfloat16)
        grad_q = (
            jnp.einsum(
                "bhck,bkhd->bchd",
                grad_scores,
                backward_key_part,
                preferred_element_type=jnp.float32,
            )
            * score_scale
        )
        grad_keys = (
            jnp.einsum("bhck,bchd->bkhd", grad_scores, queries, preferred_element_type=jnp.float32)
            * score_scale
        )
        grad_values = jnp.einsum(
            "bhck,bchd->bkhd",
            backward_weights.astype(jnp.bfloat16),
            grad_mixed,
            preferred_element_type=jnp.float32,
        )
        joined = jnp.concatenate(
            [
                grad_keys.reshape(slots_here, key_count, model_width),
                grad_values.reshape(slots_here, key_count, model_width),
            ],
            axis=-1,
        )
        grad_kv = joined
        grad_far = grad_far + diagonal_bins(
            jnp.sum(grad_scores.astype(jnp.float32), axis=0), query_pos[0], grad_far.shape[1]
        )
        grad_q, grad_kv, grad_far = (grad_q, grad_kv, grad_far)
        grad_bias_far = grad_bias_far + grad_far
        grad_kv_mine = lax.psum_scatter(
            grad_kv.astype(jnp.bfloat16), "context", scatter_dimension=1, tiled=True
        ).astype(jnp.float32)
        grad_k = grad_kv_mine[..., :model_width].astype(jnp.bfloat16)
        grad_v = grad_kv_mine[..., model_width:].astype(jnp.bfloat16)
        grad_q = grad_q.reshape(slots_here, rows_dev, model_width).astype(jnp.bfloat16)
        grad_query = grad_query + jnp.einsum(
            "bcd,bce->de", normed, grad_q, preferred_element_type=jnp.float32
        )
        grad_key = grad_key + jnp.einsum(
            "bcd,bce->de", normed, grad_k, preferred_element_type=jnp.float32
        )
        grad_value = grad_value + jnp.einsum(
            "bcd,bce->de", normed, grad_v, preferred_element_type=jnp.float32
        )
        grad_normed = jnp.einsum("bce,de->bcd", grad_q, w_query, preferred_element_type=jnp.float32)
        grad_normed = grad_normed + jnp.einsum(
            "bce,de->bcd", grad_k, w_key, preferred_element_type=jnp.float32
        )
        grad_normed = grad_normed + jnp.einsum(
            "bce,de->bcd", grad_v, w_value, preferred_element_type=jnp.float32
        )
        grad_gain_one = grad_gain_one + jnp.sum(grad_normed * inputs * scale_one, axis=(0, 1))
        input_grads.append(grad_hidden + norm_back(grad_normed, inputs, scale_one, gain_one))
    grad_in_final, grad_out_final = (grad_in_acc, grad_out_acc)
    grad_rel = jnp.dot(grad_bias_far, jnp.transpose(far_table), precision=BEST_PRECISION)
    summed = lax.psum(
        (
            grad_gain_one,
            grad_query,
            grad_key,
            grad_value,
            grad_output_w,
            grad_rel,
            grad_gain_two,
            grad_router,
        ),
        ("expert", "context", "dp"),
    )
    return (
        jnp.stack(block_outputs),
        jnp.stack(input_grads),
        summed[0],
        summed[1],
        summed[2],
        summed[3],
        summed[4],
        summed[5],
        summed[6],
        summed[7],
        grad_in_final[None],
        grad_out_final[None],
    )


F32 = jnp.float32
BF16 = jnp.bfloat16
NT = (((1,), (1,)), ((), ()))


def attention_forward_kernel(heads, dim, block, scalars, qkv, bias_rows, att, full, inv, tiles, acc, tot):
    where_z = scalars[0]
    slot_len = scalars[1]
    scale = dim ** (-0.5)
    width = heads * dim
    groups = qkv.shape[0] // block
    row = lax.broadcasted_iota(jnp.int32, (block, block), 0)
    col = lax.broadcasted_iota(jnp.int32, (block, block), 1)
    for h in range(heads):
        tiles[h] = pltpu.roll(
            jnp.broadcast_to(bias_rows[h : h + 1, :], (block, 2 * block)),
            0,
            1,
            stride=1,
            stride_axis=0,
        )

    def rows_of(group):
        return pl.ds(pl.multiple_of((group ^ where_z) * block, block), block)

    def step(q_group, k_group, kind):
        q_rows, k_rows = rows_of(q_group), rows_of(k_group)
        inside = col < slot_len - k_group * block
        if kind == 0:
            inside = inside & (col <= row)
        for h in range(heads):
            lo = h * dim
            query = qkv[q_rows, lo : lo + dim]
            key = qkv[k_rows, width + lo : width + lo + dim]
            value = qkv[k_rows, 2 * width + lo : 2 * width + lo + dim]
            scores = lax.dot_general(query, key, NT, preferred_element_type=F32) * scale
            if kind == 0:
                scores = scores + tiles[h, :, block:]
            elif kind == 1:
                scores = scores + tiles[h, :, :block]
            else:
                scores = scores + bias_rows[h : h + 1, :1]
            weights = jnp.where(inside, jnp.exp(scores), 0.0)
            part = jnp.dot(weights.astype(BF16), value, preferred_element_type=F32)
            half = weights[:, : block // 2] + weights[:, block // 2 :]
            if kind == 0:
                acc[h] = part
                tot[h] = half
            else:
                acc[h] += part
                tot[h] += half

    def q_step(q_group, carry):
        step(q_group, q_group, 0)
        lax.fori_loop(
            jnp.maximum(q_group - 1, 0), q_group, lambda k, c: (step(q_group, k, 1), c)[1], 0
        )
        lax.fori_loop(
            0, jnp.maximum(q_group - 1, 0), lambda k, c: (step(q_group, k, 2), c)[1], 0
        )
        q_rows = rows_of(q_group)
        for h in range(heads):
            lo = h * dim
            inverse = 1.0 / jnp.sum(tot[h], axis=1, keepdims=True)
            attended = acc[h] * inverse
            att[q_rows, lo : lo + dim] = attended.astype(BF16)
            full[q_rows, lo : lo + dim] = attended
            inv[q_rows, lo : lo + dim] = jnp.broadcast_to(inverse, (block, dim))
        return carry

    lax.fori_loop(0, groups, q_step, 0)


def attention_backward_kernel(
    heads,
    dim,
    block,
    scalars,
    qkv,
    grad_att,
    full,
    inv,
    bias_cols,
    grads,
    diag,
    tiles,
    bins,
    far,
    gm_ext,
    v_ext,
    key_t,
    dq_t,
    dk,
    dv,
):
    where_z = scalars[0]
    slot_len = scalars[1]
    scale = dim ** (-0.5)
    width = heads * dim
    rows = qkv.shape[0]
    groups = rows // block
    key_pos = lax.broadcasted_iota(jnp.int32, (block, block), 0)
    query_pos = lax.broadcasted_iota(jnp.int32, (block, block), 1)
    lane = lax.broadcasted_iota(jnp.int32, (rows, dim), 1)
    for h in range(heads):
        lo = h * dim
        tiles[h] = pltpu.roll(
            jnp.broadcast_to(bias_cols[h : h + 1, :], (block, 2 * block)),
            0,
            1,
            stride=1,
            stride_axis=0,
        )
        bins[h] = jnp.zeros((block, 2 * block), F32)
        far[h] = jnp.zeros((8, block), F32)
        inverse = inv[:, lo : lo + dim]
        grad = grad_att[:, lo : lo + dim]
        mixed = (grad * inverse).astype(BF16)
        total = -jnp.sum(grad * full[:, lo : lo + dim], axis=1, keepdims=True) * inverse
        first = total.astype(BF16).astype(F32)
        second = (total - first).astype(BF16).astype(F32)
        third = total - first - second
        tail = jnp.where(
            lane == 0, first, jnp.where(lane == 1, second, jnp.where(lane == 2, third, 0.0))
        )
        gm_ext[h] = jnp.concatenate([mixed, tail.astype(BF16)], axis=1)
        v_ext[h] = jnp.concatenate(
            [
                qkv[:, 2 * width + lo : 2 * width + lo + dim],
                jnp.where(lane < 3, 1.0, 0.0).astype(BF16),
            ],
            axis=1,
        )
        key_t[h] = jnp.transpose(qkv[:, width + lo : width + lo + dim].astype(F32)).astype(BF16)

    def rows_of(group):
        return pl.ds(pl.multiple_of((group ^ where_z) * block, block), block)

    def step(q_group, k_group, kind):
        q_rows, k_rows = rows_of(q_group), rows_of(k_group)
        inside = key_pos < slot_len - k_group * block
        if kind == 0:
            inside = inside & (key_pos <= query_pos)
        for h in range(heads):
            lo = h * dim
            query = qkv[q_rows, lo : lo + dim]
            key = qkv[k_rows, width + lo : width + lo + dim]
            scores = lax.dot_general(key, query, NT, preferred_element_type=F32) * scale
            if kind == 0:
                scores = scores + tiles[h, :, :block]
            elif kind == 1:
                scores = scores + tiles[h, :, block:]
            else:
                scores = scores + bias_cols[h : h + 1, 2 * block - 1 :]
            weights = jnp.where(inside, jnp.exp(scores), 0.0)
            grad_mixed = gm_ext[h, q_rows]
            grad_weights = lax.dot_general(
                v_ext[h, k_rows], grad_mixed, NT, preferred_element_type=F32
            )
            grad_scores = (weights * grad_weights).astype(BF16)
            part_q = jnp.dot(key_t[h, :, k_rows], grad_scores, preferred_element_type=F32)
            part_k = jnp.dot(grad_scores, query, preferred_element_type=F32)
            part_v = jnp.dot(weights.astype(BF16), grad_mixed, preferred_element_type=F32)
            wide = grad_scores.astype(F32)
            if kind == 0:
                dq_t[h] = part_q
                dk[h, k_rows] = part_k
                dv[h, k_rows] = part_v
                bins[h, :, :block] += wide
            else:
                dq_t[h] += part_q
                dk[h, k_rows] += part_k
                dv[h, k_rows] += part_v
                if kind == 1:
                    bins[h, :, block:] += wide
                else:
                    far[h] += jnp.sum(wide.reshape(block // 8, 8, block), axis=0)

    def q_step(q_group, carry):
        step(q_group, q_group, 0)
        lax.fori_loop(
            jnp.maximum(q_group - 1, 0), q_group, lambda k, c: (step(q_group, k, 1), c)[1], 0
        )
        lax.fori_loop(
            0, jnp.maximum(q_group - 1, 0), lambda k, c: (step(q_group, k, 2), c)[1], 0
        )
        q_rows = rows_of(q_group)
        for h in range(heads):
            lo = h * dim
            grads[q_rows, lo : lo + dim] = (jnp.transpose(dq_t[h]) * scale).astype(BF16)
        return carry

    lax.fori_loop(0, groups, q_step, 0)
    row = lax.broadcasted_iota(jnp.int32, (block, 2 * block), 0)
    for h in range(heads):
        lo = h * dim
        grads[:, width + lo : width + lo + dim] = (dk[h] * scale).astype(BF16)
        grads[:, 2 * width + lo : 2 * width + lo + dim] = dv[h, :, :dim].astype(BF16)
        skewed = bins[h]
        bit = 1
        while bit < block:
            skewed = jnp.where((row & bit) != 0, pltpu.roll(skewed, 2 * block - bit, 1), skewed)
            bit *= 2
        diag[h : h + 1, :] = jnp.sum(skewed, axis=0, keepdims=True)
        diag[4 + h : 5 + h, :block] = jnp.sum(far[h], axis=0, keepdims=True)
        diag[4 + h : 5 + h, block:] = jnp.zeros((1, block), F32)
    diag[3:4, :] = jnp.zeros((1, 2 * block), F32)
    diag[7:8, :] = jnp.zeros((1, 2 * block), F32)


VMEM_SPEC = pl.BlockSpec(memory_space=pltpu.VMEM)
SMEM_SPEC = pl.BlockSpec(memory_space=pltpu.SMEM)
KERNEL_VMEM = 40 * 1024 * 1024


def attention_forward(scalars, qkv, bias_rows, heads, dim, block):
    rows = qkv.shape[0]
    width = heads * dim
    pairs = rows * (rows + block) // 2 * heads
    return pl.pallas_call(
        functools.partial(attention_forward_kernel, heads, dim, block),
        out_shape=(
            jax.ShapeDtypeStruct((rows, width), BF16),
            jax.ShapeDtypeStruct((rows, width), F32),
            jax.ShapeDtypeStruct((rows, width), F32),
        ),
        in_specs=[SMEM_SPEC, VMEM_SPEC, VMEM_SPEC],
        out_specs=(VMEM_SPEC, VMEM_SPEC, VMEM_SPEC),
        scratch_shapes=[
            pltpu.VMEM((heads, block, 2 * block), F32),
            pltpu.VMEM((heads, block, dim), F32),
            pltpu.VMEM((heads, block, block // 2), F32),
        ],
        cost_estimate=pl.CostEstimate(
            flops=pairs * dim * 16, transcendentals=pairs, bytes_accessed=rows * width * 20
        ),
        compiler_params=pltpu.CompilerParams(vmem_limit_bytes=KERNEL_VMEM),
        name="attention_forward",
    )(scalars, qkv, bias_rows)


def attention_backward(scalars, qkv, grad_att, full, inv, bias_cols, heads, dim, block):
    rows = qkv.shape[0]
    width = heads * dim
    pairs = rows * (rows + block) // 2 * heads
    return pl.pallas_call(
        functools.partial(attention_backward_kernel, heads, dim, block),
        out_shape=(
            jax.ShapeDtypeStruct((rows, 3 * width), BF16),
            jax.ShapeDtypeStruct((8, 2 * block), F32),
        ),
        in_specs=[SMEM_SPEC] + [VMEM_SPEC] * 5,
        out_specs=(VMEM_SPEC, VMEM_SPEC),
        scratch_shapes=[
            pltpu.VMEM((heads, block, 2 * block), F32),
            pltpu.VMEM((heads, block, 2 * block), F32),
            pltpu.VMEM((heads, 8, block), F32),
            pltpu.VMEM((heads, rows, 2 * dim), BF16),
            pltpu.VMEM((heads, rows, 2 * dim), BF16),
            pltpu.VMEM((heads, dim, rows), BF16),
            pltpu.VMEM((heads, dim, block), F32),
            pltpu.VMEM((heads, rows, dim), F32),
            pltpu.VMEM((heads, rows, 2 * dim), F32),
        ],
        cost_estimate=pl.CostEstimate(
            flops=pairs * dim * 40, transcendentals=pairs, bytes_accessed=rows * width * 30
        ),
        compiler_params=pltpu.CompilerParams(vmem_limit_bytes=KERNEL_VMEM),
        name="attention_backward",
    )(scalars, qkv, grad_att, full, inv, bias_cols)


def grad_sum_kernel(part, head_part, rest_part, head_all, rest_all, head_in, rest_in, rest_out, rest_z, send, recv):
    expert = lax.axis_index("expert")
    pair = lax.axis_index("dp")
    where_z = lax.axis_index("context")
    side, core = pair // 2, pair % 2
    low, high = where_z % 2, where_z // 2

    def flip(bit, change):
        return 1 - bit if change else bit

    def rank_of(change):
        return flip(expert, change & 4) * 4 + flip(side, change & 2) * 2 + flip(core, change & 1)

    def plane_peer(change):
        return {
            "expert": flip(expert, change & 4),
            "dp": flip(side, change & 2) * 2 + flip(core, change & 1),
        }

    def z_of(change):
        return flip(high, change & 2) * 2 + flip(low, change & 1)

    def z_peer(change):
        return {"context": z_of(change)}

    barrier = pltpu.get_barrier_semaphore()
    for change in range(1, 8):
        pl.semaphore_signal(
            barrier, inc=1, device_id=plane_peer(change), device_id_type=pl.DeviceIdType.MESH
        )
    for change in range(1, 4):
        pl.semaphore_signal(
            barrier, inc=1, device_id=z_peer(change), device_id_type=pl.DeviceIdType.MESH
        )
    pl.semaphore_wait(barrier, 10)
    used = [0]
    started = []

    def push(source, target, device):
        slot = used[0]
        used[0] += 1
        copy = pltpu.make_async_remote_copy(
            src_ref=source,
            dst_ref=target,
            send_sem=send.at[slot],
            recv_sem=recv.at[slot],
            device_id=device,
            device_id_type=pl.DeviceIdType.MESH,
        )
        copy.start()
        started.append(copy)
        return copy

    me = rank_of(0)

    def rows_of(rank):
        return pl.ds(pl.multiple_of(rank * part, part), part)

    first = []
    for change in range(1, 8):
        theirs = rows_of(rank_of(change))
        first.append(push(rest_part.at[theirs], rest_in.at[change - 1], plane_peer(change)))
    for change in range(1, 8):
        theirs = rows_of(rank_of(change))
        first.append(push(head_part.at[theirs], head_in.at[change - 1], plane_peer(change)))
    for copy in first[:7]:
        copy.wait_recv()
    total = rest_part[rows_of(me), :].astype(F32)
    for i in range(7):
        total = total + rest_in[i].astype(F32)
    rest_out[0] = total.astype(BF16)
    one = push(rest_out.at[0], rest_z.at[0], z_peer(1))
    for copy in first[7:]:
        copy.wait_recv()
    total = head_part[rows_of(me), :].astype(F32)
    for i in range(7):
        total = total + head_in[i].astype(F32)
    head_all[me, where_z] = total.astype(BF16)
    along = [
        push(head_all.at[me, where_z], head_all.at[me, where_z], z_peer(change))
        for change in range(1, 4)
    ]
    one.wait_recv()
    rest_out[1] = (rest_out[0].astype(F32) + rest_z[0].astype(F32)).astype(BF16)
    two = push(rest_out.at[1], rest_z.at[1], z_peer(2))
    two.wait_recv()
    rest_all[me] = (rest_out[1].astype(F32) + rest_z[1].astype(F32)).astype(BF16)
    for copy in along:
        copy.wait_recv()
    half = part // 2
    top = pl.ds(0, half)
    bottom = pl.ds(half, half)
    head_top = pl.ds(0, 2)
    head_bottom = pl.ds(2, 2)

    def whole(rank, device):
        return [
            push(head_all.at[rank], head_all.at[rank], device),
            push(rest_all.at[rank], rest_all.at[rank], device),
        ]

    def piece(rank, head_rows, rows, device):
        return [
            push(head_all.at[rank, head_rows], head_all.at[rank, head_rows], device),
            push(rest_all.at[rank, rows], rest_all.at[rank, rows], device),
        ]

    to_x, to_y, to_core = plane_peer(4), plane_peer(2), plane_peer(1)
    by_x = whole(me, to_x)
    by_y = whole(me, to_y)
    last = whole(me, to_core)
    for copy in by_x:
        copy.wait_recv()
    on_y = piece(rank_of(4), head_top, top, to_y)
    last += whole(rank_of(4), to_core)
    for copy in by_y:
        copy.wait_recv()
    on_x = piece(rank_of(2), head_bottom, bottom, to_x)
    last += whole(rank_of(2), to_core)
    for copy in on_y:
        copy.wait_recv()
    last += piece(rank_of(6), head_top, top, to_core)
    for copy in on_x:
        copy.wait_recv()
    last += piece(rank_of(6), head_bottom, bottom, to_core)
    for copy in last:
        copy.wait_recv()
    for copy in started:
        copy.wait_send()


def grad_sum(head_part, rest_part):
    rows, head_width = head_part.shape
    rest_width = rest_part.shape[1]
    part = rows // 8
    copies = 14 + 3 + 2 + 6 + 8 + 4
    return pl.pallas_call(
        functools.partial(grad_sum_kernel, part),
        out_shape=(
            jax.ShapeDtypeStruct((8, 4, part, head_width), BF16),
            jax.ShapeDtypeStruct((8, part, rest_width), BF16),
        ),
        in_specs=[VMEM_SPEC, VMEM_SPEC],
        out_specs=(VMEM_SPEC, VMEM_SPEC),
        scratch_shapes=[
            pltpu.VMEM((7, part, head_width), BF16),
            pltpu.VMEM((7, part, rest_width), BF16),
            pltpu.VMEM((2, part, rest_width), BF16),
            pltpu.VMEM((2, part, rest_width), BF16),
            pltpu.SemaphoreType.DMA((copies,)),
            pltpu.SemaphoreType.DMA((copies,)),
        ],
        compiler_params=pltpu.CompilerParams(
            collective_id=0, has_side_effects=True, vmem_limit_bytes=KERNEL_VMEM
        ),
        name="grad_sum",
    )(head_part, rest_part)


def expert_both(rows, grad_ext, router, me, w_ins, w_outs):
    width = rows.shape[1]
    experts = router.shape[1]
    ids = lax.broadcasted_iota(jnp.int32, (1, experts), 1)
    other = grad_ext[:, width : width + 1].astype(F32).astype(jnp.int32) - me
    logits = jnp.dot(rows, router, preferred_element_type=F32)
    is_self = (ids == me).astype(F32)
    is_other = (ids == other).astype(F32)
    gap = jnp.sum(logits * (is_other - is_self), axis=1, keepdims=True)
    gate = 1.0 / (1.0 + jnp.exp(gap))
    gated = (gate * grad_ext[:, :width].astype(F32)).astype(BF16)
    acts, pres = [], []
    out = 0.0
    back = 0.0
    shift = 0.0
    for w_in, w_out in zip(w_ins, w_outs):
        pre = jnp.dot(rows, w_in, preferred_element_type=F32)
        act_full, pull = jax.vjp(jax.nn.gelu, pre)
        act = act_full.astype(BF16)
        grad_act = lax.dot_general(gated, w_out, NT, preferred_element_type=F32)
        grad_pre = pull(grad_act)[0].astype(BF16)
        shift = shift + jnp.sum(grad_act * act.astype(F32), axis=1, keepdims=True)
        out = out + jnp.dot(act, w_out, preferred_element_type=F32)
        back = back + lax.dot_general(grad_pre, w_in, NT, preferred_element_type=F32)
        acts.append(act)
        pres.append(grad_pre)
    grad_logits = ((1.0 - gate) * shift * (is_self - is_other)).astype(BF16)
    back = back + lax.dot_general(grad_logits, router, NT, preferred_element_type=F32)
    return (out * gate).astype(BF16), back.astype(BF16), gated, acts, pres, grad_logits


def after(value, other):
    return lax.optimization_barrier((value, other))[0]


def norm_scale(values):
    return lax.rsqrt(jnp.mean(values * values, axis=-1, keepdims=True) + EPSILON)


def contract_rows(left, right):
    return lax.dot_general(left, right, (((0,), (0,)), ((), ())), preferred_element_type=F32)


def local_fast(
    tokens,
    lengths,
    routes,
    attn_gain,
    w_query,
    w_key,
    w_value,
    w_output,
    rel_bias,
    ffn_gain,
    w_router,
    w_in,
    w_out,
    out_grad,
):
    micro_count, _, rows_dev, width = tokens.shape
    head_count, buckets = rel_bias.shape
    dim = width // head_count
    contexts = lax.axis_size("context")
    plane_axes = ("expert", "dp")
    plane = lax.axis_size("expert") * lax.axis_size("dp")
    heads = head_count // contexts
    head_width = heads * dim
    experts = w_router.shape[1]
    capacity = max(2, 5 * rows_dev // (2 * experts))
    pair_rows = 2 * capacity
    me = lax.axis_index(plane_axes)
    where_z = lax.axis_index("context")

    def over_z(value, k):
        return lax.ppermute(value, "context", [(i, i ^ k) for i in range(contexts)])

    def over_plane(value, k):
        return lax.ppermute(value, plane_axes, [(i, i ^ k) for i in range(plane)])

    def swap_plane(pieces):
        return jnp.concatenate(
            [pieces[0]] + [over_plane(pieces[k], k) for k in range(1, plane)], axis=-2
        )

    gain_one = attn_gain.astype(F32)
    gain_two = ffn_gain.astype(F32)
    tokens = tokens[:, 0]
    out_grad = out_grad[:, 0]
    routes = routes[:, 0]
    lengths = lengths[:, 0]

    token_blocks = []
    far = None
    for m in range(micro_count):
        far = over_z(tokens[m] if far is None else after(tokens[m], far), 2)
        near = over_z(jnp.stack([tokens[m], far]), 1)
        token_blocks.append(jnp.stack([tokens[m], near[0], far, near[1]]))

    joint = jnp.stack([w_query, w_key, w_value], axis=1).reshape(
        width, 3, contexts, head_width
    )
    w_heads = lax.dynamic_index_in_dim(joint, where_z, 2, keepdims=False).reshape(
        width, 3 * head_width
    )
    order = jnp.arange(contexts, dtype=jnp.int32) ^ where_z
    w_output_mixed = jnp.concatenate(
        [
            lax.dynamic_slice_in_dim(w_output, (where_z ^ k) * head_width, head_width, 0)
            for k in range(contexts)
        ],
        axis=0,
    )
    far_table = bucket_table(buckets, MAX_DIST)
    span = 2 * rows_dev
    distance = np.arange(span)
    table_cols = far_table[:, np.minimum(distance, MAX_DIST)]
    back_distance = np.where(distance <= rows_dev, np.minimum(rows_dev - distance, MAX_DIST), MAX_DIST)
    table_rows = far_table[:, back_distance]
    my_bias = lax.dynamic_slice_in_dim(rel_bias, where_z * heads, heads, 0)
    my_bias = jnp.pad(my_bias, ((0, 8 - heads), (0, 0)))
    bias_cols = jnp.dot(my_bias, jnp.asarray(table_cols, BF16), preferred_element_type=F32)
    bias_rows = jnp.dot(my_bias, jnp.asarray(table_rows, BF16), preferred_element_type=F32)

    query_pos = where_z * rows_dev + jnp.arange(rows_dev, dtype=jnp.int32)
    valid = query_pos[None, :] < lengths[:, None]
    order_ids = jnp.concatenate([routes[..., 0], routes[..., 1]], axis=-1)
    pair_live = jnp.concatenate([valid, valid], axis=-1)
    chosen = (
        (order_ids[..., None] == jnp.arange(experts, dtype=jnp.int32)) & pair_live[..., None]
    ).astype(jnp.int32)
    place = jnp.sum(jnp.cumsum(chosen, axis=-2) * chosen, axis=-1) - 1
    spot = jnp.where(
        pair_live & (place < capacity), (order_ids ^ me) * pair_rows + place, -pair_rows
    )
    spot = jnp.stack([spot[:, :rows_dev], spot[:, rows_dev:], routes[..., 0] + routes[..., 1]])
    spot_far = over_z(spot, 2)
    spots = jnp.stack(
        [
            jnp.concatenate([spot[0], spot_far[0] + capacity], axis=-1),
            jnp.concatenate([spot[1], spot_far[1] + capacity], axis=-1),
        ]
    )
    id_sums = jnp.concatenate([spot[2], spot_far[2]], axis=-1)
    line = jnp.arange(plane * pair_rows, dtype=jnp.int32)
    grad_far = over_z(after(out_grad, far), 2)
    picks = []
    grad_pieces = []
    for m in range(micro_count):
        pick = (
            (spots[0, m][:, None] == line[None, :]) | (spots[1, m][:, None] == line[None, :])
        ).astype(BF16)
        picks.append(pick)
        tail = jnp.pad(id_sums[m][:, None].astype(BF16), ((0, 0), (0, 127)))
        ext = jnp.concatenate(
            [jnp.concatenate([out_grad[m], grad_far[m]], axis=0), tail], axis=1
        )
        grad_pieces.append(
            contract_rows(pick, ext).astype(BF16).reshape(plane, pair_rows, width + 128)
        )
    grad_rows = swap_plane([jnp.stack([g[k] for g in grad_pieces]) for k in range(plane)])

    near_w = over_z(after(jnp.stack([w_in[0], w_out[0]]), near), 1)
    w_ins = [w_in[0], near_w[0]]
    w_outs = [w_out[0], near_w[1]]

    scalars = [jnp.stack([where_z, lengths[m]]).astype(jnp.int32) for m in range(micro_count)]
    state = []
    d_in = [0.0, 0.0]
    d_out = [0.0, 0.0]
    d_router = 0.0
    returned = []
    for m in range(micro_count):
        values = token_blocks[m].astype(F32).reshape(contexts * rows_dev, width)
        scale_one = norm_scale(values)
        normed = (values * scale_one * gain_one).astype(BF16)
        qkv = jnp.dot(normed, w_heads, preferred_element_type=F32).astype(BF16)
        att, full, inv = attention_forward(scalars[m], qkv, bias_rows, heads, dim, rows_dev)
        blocks = att.reshape(contexts, rows_dev, head_width)
        parts = [jnp.stack([blocks[0], blocks[2]])] + [
            over_z(jnp.stack([blocks[k], blocks[k ^ 2]]), k) for k in range(1, contexts)
        ]
        att_rows = jnp.concatenate(parts, axis=-1).reshape(2 * rows_dev, width)
        pair_values = jnp.concatenate([tokens[m], token_blocks[m][2]], axis=0).astype(F32)
        hidden = pair_values + jnp.dot(att_rows, w_output_mixed, preferred_element_type=F32)
        scale_two = norm_scale(hidden)
        routed = (hidden * scale_two * gain_two).astype(BF16)
        sent = contract_rows(picks[m], routed).astype(BF16).reshape(plane, pair_rows, width)
        if m:
            sent = after(sent, rows)
        rows = swap_plane([sent[k] for k in range(plane)])
        out_rows, back_rows, gated, acts, pres, grad_logits = expert_both(
            rows, grad_rows[m], w_router, me, w_ins, w_outs
        )
        back_rows = back_rows.reshape(plane, pair_rows, width)
        back = swap_plane([back_rows[k] for k in range(plane)])
        returned.append(out_rows.reshape(plane, pair_rows, width))
        for s in range(2):
            d_in[s] = d_in[s] + contract_rows(rows, pres[s])
            d_out[s] = d_out[s] + contract_rows(acts[s], gated)
        d_router = d_router + contract_rows(rows, grad_logits)
        state.append((values, scale_one, normed, qkv, full, inv, att_rows, hidden, scale_two, back))

    d_weight_far = over_z(jnp.stack([d_in[1], d_out[1]]).astype(BF16), 1)
    grad_in_final = d_in[0] + d_weight_far[0].astype(F32)
    grad_out_final = d_out[0] + d_weight_far[1].astype(F32)

    d_output = 0.0
    d_heads = 0.0
    d_gain_one = 0.0
    d_gain_two = 0.0
    d_diag = 0.0
    input_grads = []
    for m in range(micro_count):
        values, scale_one, normed, qkv, full, inv, att_rows, hidden, scale_two, back = state[m]
        grad_routed = jnp.dot(picks[m], back, preferred_element_type=F32)
        d_gain_two = d_gain_two + jnp.sum(grad_routed * hidden * scale_two, axis=0)
        live = valid[m][:, None].astype(F32)
        grad_hidden = norm_back(grad_routed, hidden, scale_two, gain_two)
        own_hidden = grad_hidden[:rows_dev] + out_grad[m].astype(F32) * live
        grad_branch = jnp.concatenate([own_hidden, grad_hidden[rows_dev:]], axis=0).astype(BF16)
        hidden_far = over_z(grad_branch[rows_dev:], 2)
        d_output = d_output + contract_rows(att_rows, grad_branch)
        sent = [
            lax.dot_general(
                grad_branch,
                w_output_mixed[k * head_width : (k + 1) * head_width],
                NT,
                preferred_element_type=F32,
            )
            .astype(BF16)
            .reshape(2, rows_dev, head_width)
            for k in range(contexts)
        ]
        got = [sent[0]] + [over_z(sent[k], k) for k in range(1, contexts)]
        grad_att = jnp.concatenate(
            [got[k][0].astype(F32) + got[k ^ 2][1].astype(F32) for k in range(contexts)], axis=0
        )
        grad_qkv, diag = attention_backward(
            scalars[m], qkv, grad_att, full, inv, bias_cols, heads, dim, rows_dev
        )
        d_diag = d_diag + diag
        d_heads = d_heads + contract_rows(normed, grad_qkv)
        partial = lax.dot_general(grad_qkv, w_heads, NT, preferred_element_type=F32).reshape(
            contexts, rows_dev, width
        )
        near = over_z(jnp.stack([partial[1], partial[3]]).astype(BF16), 1).astype(F32)
        far = over_z((partial[2] + near[1]).astype(BF16), 2).astype(F32)
        grad_normed = partial[0] + near[0] + far
        own_values = values[:rows_dev]
        own_scale = scale_one[:rows_dev]
        d_gain_one = d_gain_one + jnp.sum(grad_normed * own_values * own_scale, axis=0)
        input_grads.append(
            own_hidden
            + hidden_far.astype(F32)
            + norm_back(grad_normed, own_values, own_scale, gain_one)
        )

    out_back = swap_plane(
        [after(jnp.stack([r[k] for r in returned]), state[-1][-1]) for k in range(plane)]
    )
    mixes = [jnp.dot(picks[m], out_back[m], preferred_element_type=F32) for m in range(micro_count)]
    mix_far = over_z(jnp.stack([x[rows_dev:] for x in mixes]).astype(BF16), 2)
    block_out = jnp.stack(
        [
            jnp.where(
                valid[m][:, None],
                state[m][7][:rows_dev] + mixes[m][:rows_dev] + mix_far[m].astype(F32),
                0.0,
            ).astype(BF16)
            for m in range(micro_count)
        ]
    )

    near_bins = d_diag[:heads]
    far_bins = jnp.sum(d_diag[4 : 4 + heads], axis=1, keepdims=True) * jnp.asarray(
        far_table[:, MAX_DIST][None, :]
    )
    my_rel = (
        jnp.dot(near_bins, jnp.asarray(table_cols.T), precision=BEST_PRECISION) + far_bins
    )
    grad_rel = lax.dynamic_update_slice_in_dim(
        jnp.zeros((head_count, buckets), F32), my_rel, where_z * heads, 0
    )
    grad_output_w = jnp.concatenate(
        [
            lax.dynamic_slice_in_dim(d_output, (where_z ^ k) * head_width, head_width, 0)
            for k in range(contexts)
        ],
        axis=0,
    )
    small = jnp.concatenate(
        [d_gain_one[None], d_gain_two[None], d_router.T, jnp.pad(grad_rel.reshape(1, -1), ((0, 0), (0, width - head_count * buckets)))],
        axis=0,
    )
    rest = jnp.concatenate(
        [grad_output_w, jnp.pad(small.T, ((0, 0), (0, 128 - small.shape[0])))], axis=1
    ).astype(BF16)
    head_all, rest_all = grad_sum(d_heads.astype(BF16), rest)
    head_all = jnp.transpose(head_all, (0, 2, 1, 3)).astype(F32)
    rest_all = rest_all.reshape(width, width + 128).astype(F32)
    small = rest_all[:, width : width + 3 + experts].T

    def head_grad(i):
        return head_all[..., i * head_width : (i + 1) * head_width].reshape(width, width)

    summed = (
        small[0],
        head_grad(0),
        head_grad(1),
        head_grad(2),
        rest_all[:, :width],
        small[2 + experts, : head_count * buckets].reshape(head_count, buckets),
        small[1],
        small[2 : 2 + experts].T,
    )
    return (
        block_out[:, None],
        jnp.stack(input_grads)[:, None],
        *summed,
        grad_in_final[None],
        grad_out_final[None],
    )


def fits_fast(mesh):
    return mesh.shape["context"] == 4 and mesh.shape["expert"] * mesh.shape["dp"] == 8


def solution(mesh):
    placed = (
        P(None, ("expert", "dp"), "context", None),
        P(None, ("expert", "dp")),
        P(None, ("expert", "dp"), "context", None),
        P(),
        P(),
        P(),
        P(),
        P(),
        P(),
        P(),
        P(),
        P(("expert", "dp"), None, "context"),
        P(("expert", "dp"), "context", None),
        P(None, ("expert", "dp"), "context", None),
    )
    return jax.shard_map(
        local_fast if fits_fast(mesh) else local,
        mesh=mesh,
        in_specs=placed,
        out_specs=(
            P(None, ("expert", "dp"), "context", None),
            P(None, ("expert", "dp"), "context", None),
            P(),
            P(),
            P(),
            P(),
            P(),
            P(),
            P(),
            P(),
            P(("expert", "dp"), None, "context"),
            P(("expert", "dp"), "context", None),
        ),
        check_vma=False,
    )
```
